32 devices in a mesh: grp: 4 (over x, core), wide: 8 (over z, y).
Axes of the slice: x: 2, y: 2, z: 4, core: 2. Of those that a mesh axis runs over, the one named last changes fastest.
Arguments:
- tokens: bfloat16 [8192, 2048], P(('grp', 'wide')), may hold values from -6 to 6
- norm1_gain: bfloat16 [2048], P('wide'), may hold values from 0.5 to 1.5
- w_mix: bfloat16 [2048, 6144], P('wide'), may hold values from -0.125 to 0.125
- bound_logit: float32 [2048], P('wide'), may hold values from -2 to 8
- w_out: bfloat16 [2048, 2048], P('wide'), may hold values from -0.1875 to 0.1875
- norm2_gain: bfloat16 [2048], P('wide'), may hold values from 0.5 to 1.5
- w_glu: bfloat16 [2048, 11264], P('wide'), may hold values from -0.125 to 0.125
- w_down: bfloat16 [5632, 2048], P('wide'), may hold values from -0.109375 to 0.109375
- cotangent: bfloat16 [8192, 2048], P(('grp', 'wide')), may hold values from -6 to 6
- domain_counts: int32 [8], replicated, may hold values from 1 to 16, as said below
- domain_tags: int32 [4], replicated, may hold values from 0 to 7
Outputs:
- block_out: bfloat16 [8192, 2048], P(('grp', 'wide'))
- d_tokens: float32 [8192, 2048], P(('grp', 'wide'))
- d_norm1_gain: float32 [2048], P('wide')
- d_w_mix: float32 [2048, 6144], P('wide')
- d_bound_logit: float32 [2048], P('wide')
- d_w_out: float32 [2048, 2048], P('wide')
- d_norm2_gain: float32 [2048], P('wide')
- d_w_glu: float32 [2048, 11264], P('wide')
- d_w_down: float32 [5632, 2048], P('wide')
The draws below stay inside these ranges and needn't reach their ends.
Inputs may be any that keep to these rules, and one draw needn't show every extreme that they name: `domain_counts`: counts of different domains may differ by up to a factor of 16.
All inputs are finite; a program needn't handle non-finite values.
Results may differ from the reference program's by a relative error of at most 0.018.
Values may be sent and summed in bfloat16 or wider, within the bound.
No kernel may reach another device: no remote copies, remote signals or barrier semaphores. Data moves between devices by JAX's collectives and lax.ppermute only.
A program may use at most 448 MiB of HBM per device.

```python
import jax
import jax.numpy as jnp
from jax import lax

D = 2048
FF = 5632
SEQ_LEN = 2048
NDOM = 8
TOKENS = 8192
SEQS = 4


def draw_domain_counts(key, part):
    counts = jax.random.randint(jax.random.fold_in(key, 11), (NDOM,), 1, 17).astype(jnp.int32)
    order = jax.random.permutation(jax.random.fold_in(key, 12), NDOM).astype(jnp.int32)
    places = jnp.arange(NDOM, dtype=jnp.int32)
    counts = jnp.where(places == order[0], 16, counts)
    counts = jnp.where(places == order[1], 1, counts)
    return counts.astype(jnp.int32)


def touch_ends(drawn, own_key, least, largest):
    longest = drawn.shape.index(max(drawn.shape))
    spots = []
    for shift in (0, 1):
        where = [jax.random.randint(jax.random.fold_in(own_key, axis), (), 0, length) for axis, length in enumerate(drawn.shape)]
        where[longest] = (where[longest] + shift) % drawn.shape[longest]
        spots.append(tuple(where))
    return drawn.at[spots[0]].set(least).at[spots[1]].set(largest)


def block_scale(rng, dims, pieces, smallest, high):
    def one(dim, parts):
        heights = jax.random.uniform(jax.random.fold_in(jax.random.fold_in(rng, 6), dim), (parts,), jnp.float32, smallest / len(pieces), high / len(pieces))
        return jnp.repeat(jnp.exp(heights), dims[dim] // parts).reshape((-1,) + (1,) * (len(dims) - dim - 1))

    gain = one(*pieces[0])
    for cut in pieces[1:]:
        gain = gain * one(*cut)
    return gain


def normal_values(rng, shape, width, limit, cuts=(), held_as=jnp.bfloat16):
    loudness = block_scale(rng, shape, cuts, -0.22, 0.18) if cuts else 1.0
    drawn = jax.random.normal(rng, shape, jnp.float32) * width * loudness
    return jnp.minimum(jnp.maximum(drawn, -limit), limit).astype(held_as)


def setup_inputs(seed: int = 0) -> dict:
    keys = jax.random.split(jax.random.key(seed), 12)
    return {
        "tokens": normal_values(keys[0], (TOKENS, D), 1.0, 6.0, ((0, 32),)),
        "norm1_gain": jnp.clip(1.0 + 0.1 * jax.random.normal(keys[1], (D,), jnp.float32), 0.5, 1.5).astype(jnp.bfloat16),
        "w_mix": normal_values(keys[2], (D, 3 * D), D ** -0.5, 0.125, ((0, 8),)),
        "bound_logit": jnp.clip(-2.0 + 10.0 * jax.random.uniform(keys[3], (D,), jnp.float32) ** block_scale(keys[3], (D,), ((0, 8),), -0.2, 0.2), -2.0, 8.0),
        "w_out": normal_values(keys[4], (D, D), (D // 2) ** -0.5, 0.1875, ((0, 8),)),
        "norm2_gain": jnp.clip(1.0 + 0.1 * jax.random.normal(keys[5], (D,), jnp.float32), 0.5, 1.5).astype(jnp.bfloat16),
        "w_glu": normal_values(keys[6], (D, 2 * FF), D ** -0.5, 0.125, ((0, 8),)),
        "w_down": normal_values(keys[7], (FF, D), (FF // 2) ** -0.5, 0.109375, ((0, 8),)),
        "cotangent": normal_values(keys[8], (TOKENS, D), 1.0, 6.0, ((0, 32),)),
        "domain_counts": draw_domain_counts(jax.random.fold_in(keys[11], 71), 0),
        "domain_tags": touch_ends(jax.random.randint(keys[10], (SEQS,), 0, NDOM), jax.random.fold_in(keys[10], 1), 0, NDOM - 1).astype(jnp.int32),
    }


@jax.custom_vjp
def low(v):
    return lax.optimization_barrier(v.astype(jnp.bfloat16)).astype(jnp.float32)

@jax.custom_vjp
def low_back(v):
    return v

def low_keep(v):
    return (low(v), None)

def low_pass(kept, grad):
    return (grad,)

def back_keep(v):
    return (v, None)

def back_low(kept, grad):
    return (low(grad),)
low.defvjp(low_keep, low_pass)
low_back.defvjp(back_keep, back_low)
EPS = 1e-06

def matmul(left, right):
    return jnp.dot(left, right, precision=lax.Precision.HIGHEST, preferred_element_type=jnp.float32)

def rms_scale(values):
    return lax.rsqrt(lax.optimization_barrier(jnp.mean(values * values, axis=-1, keepdims=True)) + EPS)

def combine(earlier, later):
    return (earlier[0] * later[0], later[0] * earlier[1] + later[1])

def block_forward(params, inputs):
    gain_one, w_mix, bound_logit, w_out, gain_two, w_glu, w_down = params
    normed = low(inputs * rms_scale(inputs) * gain_one)
    mixed = low_back(matmul(normed, w_mix))
    in_part = low(mixed[:, :D])
    forget_part = low(mixed[:, D:2 * D])
    gate_part = mixed[:, 2 * D:]
    floor = jax.nn.sigmoid(bound_logit)
    forget = floor + (1.0 - floor) * jax.nn.sigmoid(forget_part)
    inflow = jax.nn.silu(in_part) * (1.0 - forget)
    _, state = lax.associative_scan(combine, (forget, inflow), axis=0)
    state = low(low_back(state))
    mixer = low(state * rms_scale(state) * jax.nn.silu(gate_part))
    middle = inputs + low_back(matmul(mixer, w_out))
    normed_two = low(middle * rms_scale(middle) * gain_two)
    gate_up = low_back(matmul(normed_two, w_glu))
    hidden = low(jax.nn.silu(gate_up[:, :FF]) * gate_up[:, FF:])
    return middle + low_back(matmul(hidden, w_down))

def reference(tokens, norm1_gain, w_mix, bound_logit, w_out, norm2_gain, w_glu, w_down, cotangent, domain_counts, domain_tags):
    params = tuple((p.astype(jnp.float32) for p in (norm1_gain, w_mix, bound_logit, w_out, norm2_gain, w_glu, w_down)))
    domains = jnp.arange(NDOM, dtype=jnp.int32)
    seq_count = lax.optimization_barrier(jnp.sum(jnp.where(domain_tags[:, None] == domains[None, :], domain_counts[None, :], 0), axis=1))
    seq_weight = 1.0 / seq_count.astype(jnp.float32)
    inputs = tokens.astype(jnp.float32).reshape(SEQS, SEQ_LEN, D)
    upstream = cotangent.astype(jnp.float32).reshape(SEQS, SEQ_LEN, D) * seq_weight[:, None, None]

    def step(totals, item):
        x_block, c_block = item
        result, pull = jax.vjp(block_forward, params, x_block)
        d_params, d_inputs = pull(c_block)
        totals = tuple((a + b for a, b in zip(totals, d_params)))
        return (totals, (result.astype(jnp.bfloat16), d_inputs))
    zeros = tuple((jnp.zeros_like(p) for p in params))
    totals, (outputs, d_inputs) = lax.scan(step, zeros, (inputs, upstream))
    block_out = outputs.reshape(TOKENS, D)
    d_tokens = d_inputs.reshape(TOKENS, D)
    return (block_out, d_tokens, totals[0], totals[1], totals[2], totals[3], totals[4], totals[5], totals[6])
```

```python
import jax
import jax.numpy as jnp
from jax import lax
from jax.experimental import pallas as pl
from jax.experimental.pallas import tpu as pltpu
from jax.sharding import PartitionSpec as P

SEQ_LEN = 2048
EPS = 1e-06
LOW = jnp.bfloat16
WIDE = jnp.float32


def contract(left, right, left_dim, right_dim):
    return lax.dot_general(
        left, right, (((left_dim,), (right_dim,)), ((), ())), preferred_element_type=WIDE
    )


def rms_scale(values):
    return lax.rsqrt(jnp.mean(values * values, axis=1, keepdims=True) + EPS)


def silu_slope(values):
    sig = jax.nn.sigmoid(values)
    return sig * (1.0 + values * (1.0 - sig))


def bits_of(size):
    count = size.bit_length() - 1
    assert size == 1 << count
    return count


def swap(value, axis, bit):
    size = lax.axis_size(axis)
    return lax.ppermute(value, axis, [(i, i ^ (1 << bit)) for i in range(size)])


def stacked(mine, other, bit_value):
    both = jnp.zeros((2,) + mine.shape, mine.dtype)
    both = lax.dynamic_update_index_in_dim(both, mine, bit_value, 0)
    return lax.dynamic_update_index_in_dim(both, other, 1 - bit_value, 0)


def bit_at(axis, bit):
    return (lax.axis_index(axis) >> bit) & 1


def gather_blocks(value, axis):
    out = value[None]
    for bit in reversed(range(bits_of(lax.axis_size(axis)))):
        other = swap(out, axis, bit)
        out = stacked(out, other, bit_at(axis, bit))
        out = out.reshape((-1,) + value.shape)
    return out


def scatter_blocks(parts, axis):
    out = parts
    for bit in range(bits_of(lax.axis_size(axis))):
        out = out.reshape((2, -1) + parts.shape[1:])
        here = bit_at(axis, bit)
        send = lax.dynamic_index_in_dim(out, 1 - here, 0, keepdims=False).astype(LOW)
        keep = lax.dynamic_index_in_dim(out, here, 0, keepdims=False)
        out = keep + swap(send, axis, bit).astype(WIDE)
    return out[0]


def sum_over(value, axis):
    for bit in range(bits_of(lax.axis_size(axis))):
        value = value + swap(value, axis, bit)
    return value


def reversed_order(size):
    count = bits_of(size)
    return [int(format(i, f"0{count}b")[::-1], 2) if count else 0 for i in range(size)]


class Ring:
    def __init__(self, axis):
        size = lax.axis_size(axis)
        order = list(range(0, size, 2)) + list(range(size - 1, 0, -2))
        self.axis, self.size = axis, size
        self.ahead = [(order[i], order[(i + 1) % size]) for i in range(size)]
        self.back = [(b, a) for a, b in self.ahead]
        index = lax.axis_index(axis)
        self.place = jnp.where(index % 2 == 0, index // 2, size - 1 - index // 2)

    def device(self, offset):
        place = (self.place + offset) % self.size
        half = (self.size + 1) // 2
        return jnp.where(place < half, 2 * place, 2 * (self.size - 1 - place) + 1)

    def gather(self, shard):
        rows, cols = shard.shape
        half = cols // 2
        fwd, bwd = shard[:, :half], shard[:, half:]
        full = jnp.zeros((rows * self.size, cols), shard.dtype)
        full = lax.dynamic_update_slice(full, shard, (self.device(0) * rows, 0))
        for step in range(1, self.size):
            fwd = lax.ppermute(fwd, self.axis, self.ahead)
            bwd = lax.ppermute(bwd, self.axis, self.back)
            full = lax.dynamic_update_slice(full, fwd, (self.device(-step) * rows, 0))
            full = lax.dynamic_update_slice(full, bwd, (self.device(step) * rows, half))
        return full

    def reduce(self, left, right):
        rows = left.shape[0] // self.size

        def block(value, offset):
            return lax.dynamic_slice_in_dim(value, self.device(offset) * rows, rows, 0)

        fwd, bwd = block(left, -1), block(right, 1)
        for step in range(1, self.size):
            fwd = lax.ppermute(fwd, self.axis, self.ahead)
            bwd = lax.ppermute(bwd, self.axis, self.back)
            fwd = (fwd.astype(WIDE) + block(left, -1 - step).astype(WIDE)).astype(LOW)
            bwd = (bwd.astype(WIDE) + block(right, 1 + step).astype(WIDE)).astype(LOW)
        return jnp.concatenate([fwd, bwd], axis=1)


LANES = 128
STEP = 16


def forget_of(zf, floor):
    sig = jax.nn.sigmoid(zf)
    return floor + (1.0 - floor) * sig, (1.0 - floor) * (1.0 - sig)


def scan_kernel(blocks, zi_ref, zf_ref, floor_ref, state_ref, decay_ref, total_ref):
    rows = zi_ref.shape[0] // blocks
    floor = floor_ref[...]
    row = lax.broadcasted_iota(jnp.int32, (8, LANES), 0)

    def step(i, carry):
        out = []
        for b in range(blocks):
            h, p = carry[b]
            at = pl.ds(pl.multiple_of(b * rows + i * STEP, STEP), STEP)
            zi = zi_ref[at, :].astype(WIDE)
            forget, rest = forget_of(zf_ref[at, :].astype(WIDE), floor)
            inflow = zi * jax.nn.sigmoid(zi) * rest
            states, decays = [], []
            for half in range(STEP // 8):
                a, v = forget[half * 8 : half * 8 + 8], inflow[half * 8 : half * 8 + 8]
                for d in (1, 2, 4):
                    v = v + a * jnp.where(row < d, 0.0, pltpu.roll(v, d, 0))
                    a = a * jnp.where(row < d, 1.0, pltpu.roll(a, d, 0))
                v = v + a * h
                a = a * p
                states.append(jnp.where(row < 1, h, pltpu.roll(v, 1, 0)))
                decays.append(jnp.where(row < 1, p, pltpu.roll(a, 1, 0)))
                h = jnp.broadcast_to(v[7:8], (8, LANES))
                p = jnp.broadcast_to(a[7:8], (8, LANES))
            state_ref[at, :] = jnp.concatenate(states, axis=0)
            decay_ref[at, :] = jnp.concatenate(decays, axis=0)
            out.append((h, p))
        return tuple(out)

    zero, one = jnp.zeros((8, LANES), WIDE), jnp.ones((8, LANES), WIDE)
    last = lax.fori_loop(0, rows // STEP, step, tuple((zero, one) for _ in range(blocks)))
    for b in range(blocks):
        total_ref[0, b : b + 1, :] = last[b][1][:1]
        total_ref[1, b : b + 1, :] = last[b][0][:1]


def back_kernel(blocks, dh_ref, zf_ref, floor_ref, adjoint_ref, decay_ref, total_ref):
    rows = dh_ref.shape[0] // blocks
    floor = floor_ref[...]
    row = lax.broadcasted_iota(jnp.int32, (8, LANES), 0)
    steps = rows // STEP

    def step(i, carry):
        out = []
        for b in range(blocks):
            m, p = carry[b]
            at = pl.ds(pl.multiple_of(b * rows + (steps - 1 - i) * STEP, STEP), STEP)
            dh = dh_ref[at, :].astype(WIDE)
            forget, _ = forget_of(zf_ref[at, :].astype(WIDE), floor)
            adjoints, decays = [], []
            for half in reversed(range(STEP // 8)):
                a, g = forget[half * 8 : half * 8 + 8], dh[half * 8 : half * 8 + 8]
                v = a * g
                for d in (1, 2, 4):
                    v = v + a * jnp.where(row >= 8 - d, 0.0, pltpu.roll(v, 8 - d, 0))
                    a = a * jnp.where(row >= 8 - d, 1.0, pltpu.roll(a, 8 - d, 0))
                v = v + a * m
                a = a * p
                adjoints.append(g + jnp.where(row >= 7, m, pltpu.roll(v, 7, 0)))
                decays.append(jnp.where(row >= 7, p, pltpu.roll(a, 7, 0)))
                m = jnp.broadcast_to(v[:1], (8, LANES))
                p = jnp.broadcast_to(a[:1], (8, LANES))
            adjoint_ref[at, :] = jnp.concatenate(adjoints[::-1], axis=0)
            decay_ref[at, :] = jnp.concatenate(decays[::-1], axis=0)
            out.append((m, p))
        return tuple(out)

    zero, one = jnp.zeros((8, LANES), WIDE), jnp.ones((8, LANES), WIDE)
    last = lax.fori_loop(0, steps, step, tuple((zero, one) for _ in range(blocks)))
    for b in range(blocks):
        total_ref[0, b : b + 1, :] = last[b][1][:1]
        total_ref[1, b : b + 1, :] = last[b][0][:1]


def chunk_scan(kernel, blocks, first, second, floor, name):
    total, chans = first.shape
    tile = pl.BlockSpec((total, LANES), lambda c: (0, c))
    return pl.pallas_call(
        lambda *refs: kernel(blocks, *refs),
        grid=(chans // LANES,),
        in_specs=[tile, tile, pl.BlockSpec((1, LANES), lambda c: (0, c))],
        out_specs=[tile, tile, pl.BlockSpec((2, blocks, LANES), lambda c: (0, 0, c))],
        out_shape=[
            jax.ShapeDtypeStruct((total, chans), WIDE),
            jax.ShapeDtypeStruct((total, chans), WIDE),
            jax.ShapeDtypeStruct((2, blocks, chans), WIDE),
        ],
        name=name,
    )(first, second, floor)


def pass_carry(totals, chunks, backward):
    size = lax.axis_size("wide")
    sign = -1 if backward else 1
    arrived = []
    for k in range(1, chunks):
        pairs = [
            (i, i + sign * k)
            for i in range(size)
            if 0 <= i + sign * k < size and (i + sign * k) // chunks == i // chunks
        ]
        arrived.append(lax.ppermute(totals, "wide", pairs))
    state = jnp.zeros_like(totals[0])
    for got in reversed(arrived):
        state = got[1] + got[0] * state
    return state


def member_columns(weight, groups, blocks, width):
    rows = weight.shape[0]
    span = width * lax.axis_size("grp")
    start = lax.axis_index("grp") * width
    pieces = [
        lax.dynamic_slice(weight, (0, i * span + start), (rows, width))
        for i in range(groups * blocks)
    ]
    return jnp.concatenate(pieces, axis=1)


def member_rows(weight):
    rows = weight.shape[0] // lax.axis_size("grp")
    return lax.dynamic_slice_in_dim(weight, lax.axis_index("grp") * rows, rows, 0)


def all_columns(parts, pieces, members):
    size, rows, cols = parts.shape
    width = cols // pieces
    at = {m: i for i, m in enumerate(members)}
    ordered = [parts[at[m], :, k * width : (k + 1) * width] for k in range(pieces) for m in range(size)]
    return jnp.concatenate(ordered, axis=1).astype(WIDE)


def all_rows(parts, members):
    at = {m: i for i, m in enumerate(members)}
    return jnp.concatenate([parts[at[m]] for m in range(len(members))], axis=0).astype(WIDE)


def body(
    tokens,
    norm1_gain,
    w_mix,
    bound_logit,
    w_out,
    norm2_gain,
    w_glu,
    w_down,
    cotangent,
    domain_counts,
    domain_tags,
):
    rows, dim = tokens.shape
    size, spread = lax.axis_size("grp"), lax.axis_size("wide")
    member, place = lax.axis_index("grp"), lax.axis_index("wide")
    members = reversed_order(size)
    own = w_mix.shape[0]
    width = own // size
    chans = dim // size
    units = w_down.shape[0] // size
    hid = units * spread
    chunks = SEQ_LEN // rows
    total = size * rows
    ring = Ring("wide")

    mix_part = member_columns(w_mix, 3, spread, width)
    glu_part = member_columns(w_glu, 2, spread, units)
    mix = ring.gather(mix_part)
    out = ring.gather(member_rows(w_out))
    down = ring.gather(member_rows(w_down))
    glu = ring.gather(glu_part)

    bound_part = lax.dynamic_slice_in_dim(bound_logit, member * width, width, 0)
    small = jnp.concatenate([norm1_gain.astype(WIDE), norm2_gain.astype(WIDE), bound_part])
    wide_order = reversed_order(spread)
    small = gather_blocks(small, "wide")
    small = jnp.stack([small[wide_order.index(i)] for i in range(spread)])
    gain_one = small[:, :own].reshape(1, dim)
    gain_two = small[:, own : 2 * own].reshape(1, dim)
    floor = jax.nn.sigmoid(small[:, 2 * own :]).reshape(1, chans)

    own_x = tokens.astype(WIDE)
    x = gather_blocks(tokens, "grp").reshape(total, dim).astype(WIDE)
    first_row = (member * spread + place) * rows
    seq = first_row // SEQ_LEN
    tag = jnp.sum(jnp.where(jnp.arange(domain_tags.shape[0]) == seq, domain_tags, 0))
    count = jnp.sum(jnp.where(jnp.arange(domain_counts.shape[0]) == tag, domain_counts, 0))
    upstream = cotangent.astype(WIDE) * (1.0 / count.astype(WIDE))
    gb = gather_blocks(upstream.astype(LOW), "grp").reshape(total, dim)

    scale_one = rms_scale(x)
    normed = (x * scale_one * gain_one).astype(LOW)
    mixed = contract(normed, mix, 1, 0)
    zi = mixed[:, :chans].astype(LOW)
    zf = mixed[:, chans : 2 * chans].astype(LOW)
    zg = mixed[:, 2 * chans :]
    prev_local, prev_decay, totals = chunk_scan(scan_kernel, size, zi, zf, floor, "scan")
    carry = pass_carry(totals, chunks, False)

    def spread_rows(per_block):
        return jnp.repeat(per_block, rows, axis=0)

    zi_f, zf_f = zi.astype(WIDE), zf.astype(WIDE)
    sig = jax.nn.sigmoid(zf_f)
    forget, rest = forget_of(zf_f, floor)
    in_act = jax.nn.silu(zi_f)
    prev = prev_local + prev_decay * spread_rows(carry)
    state = (forget * prev + in_act * rest).astype(LOW).astype(WIDE)
    gate_act = jax.nn.silu(zg)
    plain = (state * gate_act).astype(LOW)
    square = sum_over(jnp.sum(state * state, axis=1), "grp")
    scale_two = lax.rsqrt(square / dim + EPS)[:, None]
    mine = jnp.sum(jnp.where(jnp.asarray(members) == member, jnp.arange(size), 0))
    own_two = lax.dynamic_slice_in_dim(scale_two, mine * rows, rows, 0)
    branch = scatter_blocks(contract(plain, out, 1, 0).reshape(size, rows, dim), "grp")
    middle = own_x + branch * own_two
    scale_three = rms_scale(middle)
    own_normed_two = (middle * scale_three * gain_two).astype(LOW)
    normed_two = gather_blocks(own_normed_two, "grp").reshape(total, dim)

    gate = contract(normed_two, glu[:, :hid], 1, 0)
    up = contract(normed_two, glu[:, hid:], 1, 0)
    act = jax.nn.silu(gate)
    hidden = (act * up).astype(LOW)
    d_hidden = contract(gb, down, 1, 1)
    d_gate = (d_hidden * up * silu_slope(gate)).astype(LOW)
    d_up = (d_hidden * act).astype(LOW)

    d_two = contract(d_gate, glu[:, :hid], 1, 1) + contract(d_up, glu[:, hid:], 1, 1)
    d_two = scatter_blocks(d_two.reshape(size, rows, dim), "grp")
    half = dim // 2
    g_down = contract(hidden, gb, 0, 0).astype(LOW)
    g_down = ring.reduce(g_down[:, :half], g_down[:, half:])
    g_glu = ring.reduce(
        contract(normed_two, d_gate, 0, 0).astype(LOW), contract(normed_two, d_up, 0, 0).astype(LOW)
    )

    scaled = d_two * gain_two
    d_middle = (
        upstream
        + scale_three * scaled
        - middle
        * (scale_three * scale_three * scale_three)
        * jnp.mean(scaled * middle, axis=1, keepdims=True)
    )
    part_two = jnp.sum(d_two * middle * scale_three, axis=0)
    own_db = d_middle.astype(LOW)
    own_pull = jnp.sum(own_db.astype(WIDE) * branch, axis=1)
    db = gather_blocks(own_db, "grp").reshape(total, dim)
    pull = gather_blocks(own_pull, "grp").reshape(total, 1)

    d_mixer = contract(db, out, 1, 1)
    d_zg = (d_mixer * state * scale_two * silu_slope(zg)).astype(LOW)
    d_state = scale_two * (d_mixer * gate_act) - state * (
        scale_two * scale_two * scale_two * (pull / dim)
    )
    mixer = (state * scale_two * gate_act).astype(LOW)
    g_out = contract(mixer, db, 0, 0).astype(LOW)
    g_out = ring.reduce(g_out[:, :half], g_out[:, half:])

    local, decay, back_totals = chunk_scan(
        back_kernel, size, d_state.astype(LOW), zf, floor, "back_scan"
    )
    back_carry = pass_carry(back_totals, chunks, True)
    adjoint = local + decay * spread_rows(back_carry)
    d_forget = adjoint * (prev - in_act)
    d_zi = (adjoint * rest * silu_slope(zi_f)).astype(LOW)
    d_zf = (d_forget * rest * sig).astype(LOW)
    part_bound = jnp.sum(d_forget * (1.0 - sig), axis=0) * (floor * (1.0 - floor))[0]
    dz = jnp.concatenate([d_zi, d_zf, d_zg], axis=1)
    d_one = contract(dz, mix, 1, 1)
    part_one = jnp.sum(d_one * x * scale_one, axis=0)
    g_mix = contract(normed, dz, 0, 0).astype(LOW)
    cut = g_mix.shape[1] // 2
    g_mix = ring.reduce(g_mix[:, :cut], g_mix[:, cut:])
    own_d_one = scatter_blocks(d_one.reshape(size, rows, dim), "grp")
    own_scale = rms_scale(own_x)
    scaled_one = own_d_one * gain_one
    d_tokens = (
        d_middle
        + own_scale * scaled_one
        - own_x
        * (own_scale * own_scale * own_scale)
        * jnp.mean(scaled_one * own_x, axis=1, keepdims=True)
    )

    block_out = scatter_blocks(contract(hidden, down, 1, 0).reshape(size, rows, dim), "grp")
    block_out = (middle + block_out).astype(LOW)

    placed = jnp.zeros((spread, size, width), WIDE)
    placed = lax.dynamic_update_slice(
        placed, part_bound.reshape(spread, 1, width), (0, member, 0)
    ).reshape(dim)
    sums = jnp.stack([part_one, part_two, placed])
    sums = sum_over(sum_over(sums, "grp"), "wide")
    sums = lax.dynamic_slice_in_dim(sums, place * own, own, 1)

    grad_mix = all_columns(gather_blocks(g_mix, "grp"), 3 * spread, members)
    grad_glu = all_columns(gather_blocks(g_glu, "grp"), 2 * spread, members)
    grad_out = all_rows(gather_blocks(g_out, "grp"), members)
    grad_down = all_rows(gather_blocks(g_down, "grp"), members)
    return (
        block_out,
        d_tokens,
        sums[0],
        grad_mix,
        sums[2],
        grad_out,
        sums[1],
        grad_glu,
        grad_down,
    )


def solution(mesh):
    return jax.shard_map(
        body,
        mesh=mesh,
        in_specs=(
            P(("grp", "wide"), None),
            P("wide"),
            P("wide", None),
            P("wide"),
            P("wide", None),
            P("wide"),
            P("wide", None),
            P("wide", None),
            P(("grp", "wide"), None),
            P(),
            P(),
        ),
        out_specs=(
            P(("grp", "wide"), None),
            P(("grp", "wide"), None),
            P("wide"),
            P("wide", None),
            P("wide"),
            P("wide", None),
            P("wide"),
            P("wide", None),
            P("wide", None),
        ),
        check_vma=False,
    )
```
